128 devices in a mesh: row: 32 (over x, y, core), col: 4 (over z).
Axes of the slice: x: 4, y: 4, z: 4, core: 2. Of those that a mesh axis runs over, the one named last changes fastest.
Arguments:
- frames: float32 [64, 65536], P(None, ('row', 'col')), may hold values from -8 to 8
- start: float32 [32, 65536], P(None, ('row', 'col')), may hold values from -6 to 6
Outputs:
- basis: float32 [32, 65536], P(None, ('row', 'col'))
The draws below stay inside these ranges and needn't reach their ends.
All inputs are finite; a program needn't handle non-finite values.
Results may differ from the reference program's by a relative error of at most 0.0003.
Values sent between devices are 32-bit elements; how exact they have to be, the bound alone decides.
A program may use at most 320 MiB of HBM per device.

```python
import math
import jax
import jax.numpy as jnp
from jax import lax

F = 64
KV = 32
FRAMES = 65536


def draw_frames(key, part):
    first_key, second_key, third_key, fourth_key = jax.random.split(key, 4)
    groups = 16
    labels = jax.random.randint(first_key, (FRAMES,), 0, groups)
    centers = jax.random.truncated_normal(second_key, -4.0, 4.0, (F, groups), jnp.float32)
    noise = jax.random.truncated_normal(third_key, -4.0, 4.0, (F, FRAMES), jnp.float32)
    spread = jnp.exp(jax.random.uniform(fourth_key, (FRAMES,), jnp.float32, math.log(0.3), math.log(1.0)))
    picked = jnp.take(centers, labels, axis=1)
    return picked + spread[None, :] * noise


def shard_levels(rng, extent, pieces, least, top_value):
    level, own = 1.0, jax.random.fold_in(rng, 6)
    for axis_at, blocks in pieces:
        steps = jnp.exp(jax.random.uniform(jax.random.fold_in(own, axis_at), (blocks,), jnp.float32, least / len(pieces), top_value / len(pieces)))
        level = level * jnp.repeat(steps, extent[axis_at] // blocks).reshape([-1 if axis == axis_at else 1 for axis in range(len(extent))])
    return level


def gaussian(stream_key, shape, width, most, cuts=(), kind=jnp.bfloat16):
    entries = width * jax.random.normal(stream_key, shape, jnp.float32)
    if cuts:
        entries = entries * shard_levels(stream_key, shape, cuts, -0.22, 0.18)
    return jnp.clip(entries, -most, most).astype(kind)


def setup_inputs(seed: int = 0) -> dict:
    arg_keys = jax.random.split(jax.random.key(seed), 3)
    return {
        "frames": draw_frames(jax.random.fold_in(arg_keys[2], 71), 0),
        "start": gaussian(arg_keys[1], (KV, FRAMES), 1.0, 6.0, ((1, 128),), jnp.float32),
    }


def build_block(block_points, block_squares, column_points, column_squares):
    products = lax.dot_general(block_points, column_points, (((0,), (0,)), ((), ())), precision=lax.Precision.HIGHEST)
    distance = block_squares[:, None] + column_squares[None, :] - 2.0 * products
    return jnp.exp(-distance / (0.5 * block_points.shape[0]))

def orthonormal(vectors):
    gram_matrix = jnp.dot(vectors, vectors.T, precision=lax.Precision.HIGHEST) / FRAMES
    factor = jnp.linalg.cholesky(gram_matrix)
    return jax.scipy.linalg.solve_triangular(factor, vectors, lower=True)

def reference(frames, start):
    block_size = math.gcd(FRAMES, 1024)
    block_count = FRAMES // block_size
    squares = jnp.sum(frames * frames, axis=0)
    indices = jnp.arange(block_count, dtype=jnp.int32)

    def kernel_part(index):
        first = (index * block_size).astype(jnp.int32)
        points = lax.dynamic_slice_in_dim(frames, first, block_size, 1)
        point_squares = lax.dynamic_slice_in_dim(squares, first, block_size, 0)
        return build_block(points, point_squares, frames, squares)

    def density_part(index):
        return jnp.sum(kernel_part(index), axis=1)
    density = lax.map(density_part, indices).reshape(FRAMES)
    inverse = 1.0 / density

    def degree_part(index):
        return jnp.dot(kernel_part(index), inverse, precision=lax.Precision.HIGHEST)
    degree = lax.map(degree_part, indices).reshape(FRAMES)

    def markov(vectors):
        scaled = vectors * inverse[None, :]

        def product_part(index):
            return lax.dot_general(scaled, kernel_part(index), (((1,), (1,)), ((), ())), precision=lax.Precision.HIGHEST)
        blocks = lax.map(product_part, indices)
        joined = jnp.transpose(blocks, (1, 0, 2)).reshape(vectors.shape[0], FRAMES)
        return joined / degree[None, :]
    grown_one = markov(start)
    basis_one = orthonormal(grown_one)
    grown_two = markov(basis_one)
    return orthonormal(grown_two)
```

```python
import math

import jax
import jax.numpy as jnp
from jax import lax
from jax.experimental import pallas as pl
from jax.experimental.pallas import tpu as pltpu
from jax.sharding import PartitionSpec as P

MESH = pl.DeviceIdType.MESH
BF = jnp.bfloat16
F8 = jnp.float8_e4m3fn
F32 = jnp.float32
LOW_SCALE = 2.0**17
STAGES = 3
KEPT = (2, 4, 6)
SENT = (0, 1, 3, 5, 7)


def features(points, stationary):
    scaled = points * math.sqrt(math.log2(math.e) / 16.0 * (64.0 / points.shape[0]))
    high = scaled.astype(BF)
    low = (scaled - high.astype(F32)).astype(BF)
    half = 0.5 * jnp.sum(scaled * scaled, axis=0, keepdims=True)
    one = half.astype(BF).astype(F32)
    two = (half - one).astype(BF).astype(F32)
    three = half - one - two
    row = lax.broadcasted_iota(jnp.int32, (16, points.shape[1]), 0)
    unit = jnp.ones_like(one)
    if stationary:
        first, rest, middle = (-one, -two, -three), (-unit, -unit, -unit), (high, high, low)
    else:
        first, rest, middle = (unit, unit, unit), (one, two, three), (high, low, high)
    extra = jnp.zeros((16, points.shape[1]), F32)
    for index, value in enumerate(first + rest):
        extra = jnp.where(row == index, value, extra)
    pad = jnp.zeros((48, points.shape[1]), BF)
    return jnp.concatenate(middle + (extra.astype(BF), pad), axis=0)


def inverse_factor(gram):
    n = gram.shape[0]
    row = lax.broadcasted_iota(jnp.int32, (n, n), 0)
    column = lax.broadcasted_iota(jnp.int32, (n, n), 1)
    inverse = jnp.where(row == column, 1.0, 0.0).astype(F32)
    for c in range(n):
        pivot = gram[c : c + 1, c : c + 1]
        root = lax.rsqrt(pivot)
        root = root * (1.5 - 0.5 * pivot * root * root)
        line = gram[c : c + 1, :] * root
        line_inverse = inverse[c : c + 1, :] * root
        factor = jnp.where(row[:, :1] > c, gram[:, c : c + 1] * root, 0.0)
        gram = jnp.where(row == c, line, gram - factor * line)
        inverse = jnp.where(row == c, line_inverse, inverse - factor * line_inverse)
    return inverse


def kernel(
    X, Z, frames, start, out, far_high, far_low,
    near_high, near_low, stage_high, stage_low, zframes, fall, sall, gall, iall, stat, turned,
    acc, low_acc, dacc, part, dgot, got_one, got_two, degree, gram_part, gram_all, gram_sum, gram_col, ready,
    f_recv, s_recv, g_recv, zf_recv, d_recv, i_recv, one_recv, two_recv, p_recv, q_recv,
    send, forward, write_sem, read_sem,
):
    NO = X * X
    NB = 2 * NO
    B = frames.shape[1]
    R = Z * B
    V = start.shape[0]
    NH = len(SENT) * (NB // 8)
    total = X * X * 2 * Z * B
    me, z = lax.axis_index("row"), lax.axis_index("col")
    core, chip = lax.rem(me, 2), me // 2
    cx, cy = chip // X, lax.rem(chip, X)

    def plane(o):
        return {"row": (lax.rem(cx + o // X, X) * X + lax.rem(cy + lax.rem(o, X), X)) * 2 + core, "col": z}

    def back(o):
        return lax.rem(X - o // X, X) * X + lax.rem(X - lax.rem(o, X), X)

    sibling = {"row": chip * 2 + 1 - core, "col": z}

    def along(dz):
        return {"row": me, "col": lax.rem(z + dz, Z)}

    def post(d):
        return {"row": chip * 2 + lax.rem(core + d // Z, 2), "col": lax.rem(z + lax.rem(d, Z), Z)}

    def post_back(d):
        return (d // Z) * Z + lax.rem(Z - lax.rem(d, Z), Z)

    def push(src, dst, send_sem, recv_sem, device):
        pltpu.make_async_remote_copy(
            src_ref=src, dst_ref=dst, send_sem=send_sem, recv_sem=recv_sem, device_id=device, device_id_type=MESH
        ).start()

    def arrived(ref, sem):
        pltpu.make_async_remote_copy(
            src_ref=ref, dst_ref=ref, send_sem=send.at[0], recv_sem=sem, device_id=sibling, device_id_type=MESH
        ).wait_recv()

    def left(ref, sem):
        pltpu.make_async_remote_copy(
            src_ref=ref, dst_ref=ref, send_sem=sem, recv_sem=f_recv.at[0], device_id=sibling, device_id_type=MESH
        ).wait_send()

    def gather_start(mine, buffer, recv, sem, forward_sem):
        push(mine, buffer.at[1], forward_sem, recv.at[1], sibling)

        def each(o, _):
            slot = 2 * back(o)
            push(mine, buffer.at[slot], sem, recv.at[slot], plane(o))
            return 0

        lax.fori_loop(1, NO, each, 0)

    def pass_on(o, buffer, recv, forward_sem):
        arrived(buffer.at[2 * o], recv.at[2 * o])
        push(buffer.at[2 * o], buffer.at[2 * o + 1], forward_sem, recv.at[2 * o + 1], sibling)

    def gather_end(buffer, sem, forward_sem):
        left(buffer.at[pl.ds(0, NO - 1)], sem)
        left(buffer.at[pl.ds(0, NO)], forward_sem)

    def col_sum_start(source, target, recv, sem):
        for dz in range(1, Z):
            push(source.at[dz], target.at[Z - dz], sem, recv.at[Z - dz], along(dz))

    barrier = pltpu.get_barrier_semaphore()

    def greet_plane(o, _):
        pl.semaphore_signal(barrier, inc=1, device_id=plane(o), device_id_type=MESH)
        return 0

    def greet_post(d, _):
        pl.semaphore_signal(barrier, inc=1, device_id=post(d), device_id_type=MESH)
        return 0

    lax.fori_loop(1, NO, greet_plane, 0)
    lax.fori_loop(1, 2 * Z, greet_post, 0)
    pl.semaphore_wait(barrier, NO - 1 + 2 * Z - 1)

    for dz in range(1, Z):
        push(frames, zframes.at[Z - dz], send.at[1], zf_recv.at[Z - dz], along(dz))
    gather_start(frames, fall, f_recv, send.at[0], forward.at[0])
    gather_start(start, sall, s_recv, send.at[2], forward.at[1])
    fall[0] = frames[...]
    sall[0] = start[...]
    dacc[...] = jnp.zeros_like(dacc)
    stat[:, 0:B] = features(frames[...], True)
    for dz in range(1, Z):
        arrived(zframes.at[dz], zf_recv.at[dz])
        stat[:, dz * B : (dz + 1) * B] = features(zframes[dz], True)

    def writes(h):
        slot = lax.rem(h, STAGES)
        return (
            pltpu.make_async_copy(stage_high.at[slot], far_high.at[h], write_sem.at[slot, 0]),
            pltpu.make_async_copy(stage_low.at[slot], far_low.at[h], write_sem.at[slot, 1]),
        )

    def reads(h):
        slot = lax.rem(h, STAGES)
        return (
            pltpu.make_async_copy(far_high.at[h], stage_high.at[slot], read_sem.at[slot, 0]),
            pltpu.make_async_copy(far_low.at[h], stage_low.at[slot], read_sem.at[slot, 1]),
        )

    width = min(512, R)

    def build(n, high_ref, low_ref):
        turned[...] = features(fall[n], False).T
        for c in range(R // width):
            at = slice(c * width, (c + 1) * width)
            power = jnp.dot(turned[...], stat[:, at], preferred_element_type=F32)
            value = jnp.exp2(power)
            high = value.astype(BF)
            high_ref[:, at] = high
            low_ref[:, at] = ((value - high.astype(F32)) * LOW_SCALE).astype(F8)
            dacc[:, at] += jnp.sum(value.reshape(B // 8, 8, width), axis=0)

    def build_group(g, _):
        for i in range(8):
            n = g * 8 + i
            if i % 2 == 0:
                o = g * 4 + i // 2

                @pl.when(o + 1 < NO)
                def _():
                    pass_on(o + 1, fall, f_recv, forward.at[0])
            else:
                arrived(fall.at[n], f_recv.at[n])
            if i in KEPT:
                at = g * len(KEPT) + KEPT.index(i)
                build(n, near_high.at[at], near_low.at[at])
            else:
                h = g * len(SENT) + SENT.index(i)

                @pl.when(h >= STAGES)
                def _():
                    for copy in writes(h - STAGES):
                        copy.wait()

                slot = lax.rem(h, STAGES)
                build(n, stage_high.at[slot], stage_low.at[slot])
                for copy in writes(h):
                    copy.start()
        return 0

    lax.fori_loop(0, NB // 8, build_group, 0)

    for dz in range(Z):
        part[dz, 0:8, :] = dacc[:, dz * B : (dz + 1) * B]
    for dz in range(1, Z):
        push(part.at[dz, pl.ds(0, 8)], dgot.at[Z - dz], send.at[3], d_recv.at[Z - dz], along(dz))
    for h in range(NH - STAGES, NH):
        for copy in writes(h):
            copy.wait()
    for h in range(STAGES):
        for copy in reads(h):
            copy.start()

    def pass_start(o, _):
        pass_on(o, sall, s_recv, forward.at[1])
        return 0

    lax.fori_loop(1, NO, pass_start, 0)
    dgot[0] = part[0, 0:8, :]
    for dz in range(1, Z):
        arrived(dgot.at[dz], d_recv.at[dz])
    density = jnp.sum(dgot[0] + dgot[1] if Z == 2 else dgot[0] + dgot[1] + dgot[2] + dgot[3], axis=0, keepdims=True)
    iall[0] = jnp.broadcast_to(1.0 / density, (8, B))
    push(iall.at[0], iall.at[1], forward.at[2], i_recv.at[0], sibling)
    arrived(iall.at[1], i_recv.at[0])

    def send_inverse(o, _):
        slot = back(o)
        push(iall.at[pl.ds(0, 2)], iall.at[pl.ds(2 * slot, 2)], send.at[4], i_recv.at[slot], plane(o))
        return 0

    lax.fori_loop(1, NO, send_inverse, 0)
    acc[...] = jnp.zeros_like(acc)
    low_acc[...] = jnp.zeros_like(low_acc)
    gather_end(fall, send.at[0], forward.at[0])
    gather_end(sall, send.at[2], forward.at[1])
    left(zframes.at[pl.ds(0, Z - 1)], send.at[1])
    left(dgot.at[pl.ds(0, Z - 1)], send.at[3])

    def take_inverse(o, _):
        arrived(iall.at[pl.ds(2 * o, 2)], i_recv.at[o])
        return 0

    lax.fori_loop(1, NO, take_inverse, 0)
    largest = jnp.max(jnp.max(jnp.max(iall[...], axis=0), axis=0, keepdims=True), axis=1, keepdims=True)
    low_weight = 400.0 / (6.0 * largest)

    def sweep(n, vectors, with_degree, high_ref, low_ref):
        inverse = iall[n]
        weights = vectors[n] * inverse[0:1, :]
        high = weights.astype(BF)
        low = (weights - high.astype(F32)).astype(BF)
        rows = 2 * V
        pieces = [high, low]
        if with_degree:
            inverse_high = inverse.astype(BF)
            pieces += [jnp.concatenate([inverse_high.astype(F32), inverse - inverse_high.astype(F32)], axis=0).astype(BF)]
            rows += 16
        spread = jnp.concatenate(pieces, axis=0)
        acc[0:rows, :] += jnp.dot(spread, high_ref[...], preferred_element_type=F32)
        low_acc[...] += jnp.dot((weights * low_weight).astype(F8), low_ref[...], preferred_element_type=F32)

    def sweep_group(vectors, recv, with_degree, last, g, _):
        for i in range(8):
            n = g * 8 + i
            if i % 2 == 1:
                arrived(vectors.at[n], recv.at[n])
            elif last:
                o = g * 4 + i // 2

                @pl.when(o + 1 < NO)
                def _():
                    pass_on(o + 1, vectors, recv, forward.at[3])

            if i in KEPT:
                at = g * len(KEPT) + KEPT.index(i)
                sweep(n, vectors, with_degree, near_high.at[at], near_low.at[at])
            else:
                h = g * len(SENT) + SENT.index(i)
                for copy in reads(h):
                    copy.wait()
                slot = lax.rem(h, STAGES)
                sweep(n, vectors, with_degree, stage_high.at[slot], stage_low.at[slot])

                @pl.when(h + STAGES < NH)
                def _():
                    for copy in reads(h + STAGES):
                        copy.start()

        return 0

    def own_sum(got, recv, sem, with_degree):
        for dz in range(Z):
            at = slice(dz * B, (dz + 1) * B)
            part[dz, 0:V, :] = acc[0:V, at] + acc[V : 2 * V, at] + low_acc[:, at] * (1.0 / (low_weight * LOW_SCALE))
            if with_degree:
                part[dz, V : V + 8, :] = acc[2 * V : 2 * V + 8, at] + acc[2 * V + 8 : 2 * V + 16, at]
        col_sum_start(part, got, recv, sem)

    def own_total(got, recv):
        result = part[0]
        for dz in range(1, Z):
            arrived(got.at[dz], recv.at[dz])
            result = result + got[dz]
        return result

    def gram_of(vectors):
        return lax.dot_general(
            vectors, vectors, (((1,), (1,)), ((), ())), precision=lax.Precision.HIGHEST, preferred_element_type=F32
        ) * (1.0 / total)

    def gram_send(which, vectors):
        gram_all[which, 0] = gram_of(vectors)

        def each(o, _):
            slot = back(o)
            push(gram_all.at[which, 0], gram_all.at[which, slot], send.at[5 + which], p_recv.at[which, slot], plane(o))
            return 0

        lax.fori_loop(1, NO, each, 0)

    def gram_turn(which):
        def each(o, _):
            arrived(gram_all.at[which, o], p_recv.at[which, o])
            return 0

        lax.fori_loop(1, NO, each, 0)
        gram_col[which, 0] = jnp.sum(gram_all[which], axis=0)

        def out_to(d, _):
            slot = post_back(d)
            push(gram_col.at[which, 0], gram_col.at[which, slot], send.at[7 + which], q_recv.at[which, slot], post(d))
            return 0

        lax.fori_loop(1, 2 * Z, out_to, 0)

    def gram_total(which):
        def each(d, _):
            arrived(gram_col.at[which, d], q_recv.at[which, d])
            return 0

        lax.fori_loop(1, 2 * Z, each, 0)
        return jnp.sum(gram_col[which], axis=0)

    def gram_end(which):
        left(gram_all.at[which, pl.ds(0, NO - 1)], send.at[5 + which])
        left(gram_col.at[which, pl.ds(0, 2 * Z - 1)], send.at[7 + which])

    lax.fori_loop(0, NB // 8, lambda g, c: sweep_group(sall, s_recv, True, False, g, c), 0)
    for h in range(STAGES):
        for copy in reads(h):
            copy.start()
    own_sum(got_one, one_recv, send.at[9], True)
    acc[...] = jnp.zeros_like(acc)
    low_acc[...] = jnp.zeros_like(low_acc)
    left(iall.at[0], forward.at[2])
    left(iall.at[pl.ds(0, 2 * (NO - 1))], send.at[4])
    result = own_total(got_one, one_recv)
    degree[...] = result[V : V + 8, :]
    grown = result[0:V, :] / degree[0:1, :]
    gall[0] = grown
    gather_start(gall.at[0], gall, g_recv, send.at[10], forward.at[3])
    gram_send(0, grown)
    left(part.at[pl.ds(0, Z - 1)], send.at[9])

    def second_group(g, c):
        @pl.when(g == NB // 8 - 1)
        def _():
            gram_turn(0)

        return sweep_group(gall, g_recv, False, True, g, c)

    lax.fori_loop(0, NB // 8, second_group, 0)
    own_sum(got_two, two_recv, send.at[11], False)
    first = inverse_factor(gram_total(0))
    result = own_total(got_two, two_recv)
    grown_two = result[0:V, :] / degree[0:1, :]
    grown_two = jnp.dot(first, grown_two, precision=lax.Precision.HIGHEST, preferred_element_type=F32)
    gram_send(1, grown_two)
    gather_end(gall, send.at[10], forward.at[3])
    left(part.at[pl.ds(0, Z - 1)], send.at[11])
    gram_end(0)
    gram_turn(1)
    second = inverse_factor(gram_total(1))
    out[...] = jnp.dot(second, grown_two, precision=lax.Precision.HIGHEST, preferred_element_type=F32)
    gram_end(1)


def solution(mesh):
    X = math.isqrt(mesh.shape["row"] // 2)
    Z = mesh.shape["col"]
    NO, NB = X * X, 2 * X * X

    def step(frames, start):
        F, B = frames.shape
        V = start.shape[0]
        R = Z * B
        near, far = len(KEPT) * (NB // 8), len(SENT) * (NB // 8)
        vmem = pl.BlockSpec(memory_space=pltpu.VMEM)
        hbm = pl.BlockSpec(memory_space=pltpu.HBM)
        dma = pltpu.SemaphoreType.DMA
        basis, _, _ = pl.pallas_call(
            lambda *refs: kernel(X, Z, *refs),
            out_shape=(
                jax.ShapeDtypeStruct((V, B), F32),
                jax.ShapeDtypeStruct((far, B, R), BF),
                jax.ShapeDtypeStruct((far, B, R), F8),
            ),
            in_specs=[vmem, vmem],
            out_specs=(vmem, hbm, hbm),
            scratch_shapes=[
                pltpu.VMEM((near, B, R), BF),
                pltpu.VMEM((near, B, R), F8),
                pltpu.VMEM((STAGES, B, R), BF),
                pltpu.VMEM((STAGES, B, R), F8),
                pltpu.VMEM((Z, F, B), F32),
                pltpu.VMEM((NB, F, B), F32),
                pltpu.VMEM((NB, V, B), F32),
                pltpu.VMEM((NB, V, B), F32),
                pltpu.VMEM((NB, 8, B), F32),
                pltpu.VMEM((256, R), BF),
                pltpu.VMEM((B, 256), BF),
                pltpu.VMEM((2 * V + 16, R), F32),
                pltpu.VMEM((V, R), F32),
                pltpu.VMEM((8, R), F32),
                pltpu.VMEM((Z, V + 8, B), F32),
                pltpu.VMEM((Z, 8, B), F32),
                pltpu.VMEM((Z, V + 8, B), F32),
                pltpu.VMEM((Z, V + 8, B), F32),
                pltpu.VMEM((8, B), F32),
                pltpu.VMEM((V, V), F32),
                pltpu.VMEM((2, NO, V, V), F32),
                pltpu.VMEM((V, V), F32),
                pltpu.VMEM((2, 2 * Z, V, V), F32),
                pltpu.VMEM((V, V), F32),
                dma((NB,)), dma((NB,)), dma((NB,)),
                dma((Z,)), dma((Z,)), dma((NO,)), dma((Z,)), dma((Z,)),
                dma((2, NO)), dma((2, 2 * Z)),
                dma((12,)), dma((4,)), dma((STAGES, 2)), dma((STAGES, 2)),
            ],
            compiler_params=pltpu.CompilerParams(
                collective_id=0, has_side_effects=True, vmem_limit_bytes=64 * 1024 * 1024 - 512 * 1024
            ),
            name="diffusion",
        )(frames, start)
        return basis

    return jax.shard_map(
        step,
        mesh=mesh,
        in_specs=(P(None, ("row", "col")), P(None, ("row", "col"))),
        out_specs=P(None, ("row", "col")),
        check_vma=False,
    )
```

```python
import math

import jax
import jax.numpy as jnp
from jax import lax
from jax.experimental import pallas as pl
from jax.experimental.pallas import tpu as pltpu
from jax.sharding import PartitionSpec as P

MESH = pl.DeviceIdType.MESH
BF = jnp.bfloat16
F8 = jnp.float8_e4m3fn
F32 = jnp.float32
SHIFT = 17
STAGES = 6
KEPT = (2, 4, 6)
SENT = (0, 1, 3, 5, 7)


def features(points, stationary):
    scaled = points * math.sqrt(math.log2(math.e) / 16.0 * (64.0 / points.shape[0]))
    high = scaled.astype(BF)
    low = (scaled - high.astype(F32)).astype(BF)
    half = 0.5 * jnp.sum(scaled * scaled, axis=0, keepdims=True)
    half = SHIFT - half if stationary else half
    one = half.astype(BF).astype(F32)
    two = (half - one).astype(BF).astype(F32)
    three = half - one - two
    row = lax.broadcasted_iota(jnp.int32, (16, points.shape[1]), 0)
    unit = jnp.ones_like(one)
    if stationary:
        first, rest, middle = (one, two, three), (-unit, -unit, -unit), (high, high, low)
    else:
        first, rest, middle = (unit, unit, unit), (one, two, three), (high, low, high)
    extra = jnp.zeros((16, points.shape[1]), F32)
    for index, value in enumerate(first + rest):
        extra = jnp.where(row == index, value, extra)
    pad = jnp.zeros((48, points.shape[1]), BF)
    return jnp.concatenate(middle + (extra.astype(BF), pad), axis=0)


def inverse_factor(gram):
    n = gram.shape[0]
    row = lax.broadcasted_iota(jnp.int32, (n, n), 0)
    column = lax.broadcasted_iota(jnp.int32, (n, n), 1)
    inverse = jnp.where(row == column, 1.0, 0.0).astype(F32)
    for c in range(n):
        pivot = gram[c : c + 1, c : c + 1]
        root = lax.rsqrt(pivot)
        root = root * (1.5 - 0.5 * pivot * root * root)
        line = gram[c : c + 1, :] * root
        line_inverse = inverse[c : c + 1, :] * root
        factor = jnp.where(row[:, :1] > c, gram[:, c : c + 1] * root, 0.0)
        gram = jnp.where(row == c, line, gram - factor * line)
        inverse = jnp.where(row == c, line_inverse, inverse - factor * line_inverse)
    return inverse


def kernel(
    X, Z, frames, start, out, far_high, far_low,
    near_high, near_low, stage_high, stage_low, zframes, fall, sall, gall, iall, stat, turned,
    acc, low_acc, dacc, part, line_part, dgot, line_got, got_one, got_two, degree, gram_all, gram_col,
    f_recv, s_recv, g_recv, zf_recv, d_recv, line_recv, i_recv, one_recv, two_recv, p_recv, q_recv,
    send, forward, write_sem, read_sem,
):
    NO = X * X
    NB = 2 * NO
    B = frames.shape[1]
    R = Z * B
    V = start.shape[0]
    NH = len(SENT) * (NB // 8)
    total = X * X * 2 * Z * B
    me, z = lax.axis_index("row"), lax.axis_index("col")
    core, chip = lax.rem(me, 2), me // 2
    cx, cy = chip // X, lax.rem(chip, X)

    rows_x = [lax.rem(cx + d, X) * (2 * X) + core for d in range(X)]
    rows_y = [lax.rem(cy + d, X) * 2 for d in range(X)]

    def plane(o):
        return {"row": rows_x[(X - o // X) % X] + rows_y[(X - o % X) % X], "col": z}

    sibling = {"row": chip * 2 + 1 - core, "col": z}

    cols = [lax.rem(z + d, Z) for d in range(Z)]

    def along(dz):
        return {"row": me, "col": cols[dz]}

    def post(d):
        return {"row": me if d < Z else chip * 2 + 1 - core, "col": cols[(Z - d % Z) % Z]}

    def push(src, dst, send_sem, recv_sem, device):
        pltpu.make_async_remote_copy(
            src_ref=src, dst_ref=dst, send_sem=send_sem, recv_sem=recv_sem, device_id=device, device_id_type=MESH
        ).start()

    def arrived(ref, sem):
        pltpu.make_async_remote_copy(
            src_ref=ref, dst_ref=ref, send_sem=send.at[0], recv_sem=sem, device_id=sibling, device_id_type=MESH
        ).wait_recv()

    def left(ref, sem):
        pltpu.make_async_remote_copy(
            src_ref=ref, dst_ref=ref, send_sem=sem, recv_sem=f_recv.at[0], device_id=sibling, device_id_type=MESH
        ).wait_send()

    def gather_start(mine, buffer, recv, sem, forward_sem):
        push(mine, buffer.at[1], forward_sem, recv.at[1], sibling)
        for o in range(1, NO):
            push(mine, buffer.at[2 * o], sem, recv.at[2 * o], plane(o))

    def pass_on(o, buffer, recv, forward_sem):
        arrived(buffer.at[2 * o], recv.at[2 * o])
        push(buffer.at[2 * o], buffer.at[2 * o + 1], forward_sem, recv.at[2 * o + 1], sibling)

    def gather_end(buffer, sem, forward_sem):
        left(buffer.at[pl.ds(0, NO - 1)], sem)
        left(buffer.at[pl.ds(0, NO)], forward_sem)

    barrier = pltpu.get_barrier_semaphore()

    for o in range(1, NO):
        pl.semaphore_signal(barrier, inc=1, device_id=plane(o), device_id_type=MESH)
    for d in range(1, 2 * Z):
        pl.semaphore_signal(barrier, inc=1, device_id=post(d), device_id_type=MESH)
    pl.semaphore_wait(barrier, NO - 1 + 2 * Z - 1)

    for dz in range(1, Z):
        push(frames, zframes.at[Z - dz], send.at[1], zf_recv.at[Z - dz], along(dz))
    gather_start(frames, fall, f_recv, send.at[0], forward.at[0])
    gather_start(start, sall, s_recv, send.at[2], forward.at[1])
    fall[0] = frames[...]
    sall[0] = start[...]
    dacc[...] = jnp.zeros_like(dacc)
    stat[:, 0:B] = features(frames[...], True)
    for dz in range(1, Z):
        arrived(zframes.at[dz], zf_recv.at[dz])
        stat[:, dz * B : (dz + 1) * B] = features(zframes[dz], True)

    def writes(h, half):
        slot = lax.rem(2 * h + half, STAGES)
        return (
            pltpu.make_async_copy(stage_high.at[slot], far_high.at[half * NH + h], write_sem.at[slot, 0]),
            pltpu.make_async_copy(stage_low.at[slot], far_low.at[half * NH + h], write_sem.at[slot, 1]),
        )

    def reads(t):
        slot = lax.rem(t, STAGES)
        at = lax.rem(t + NH, 2 * NH)
        return (
            pltpu.make_async_copy(far_high.at[at], stage_high.at[slot], read_sem.at[slot, 0]),
            pltpu.make_async_copy(far_low.at[at], stage_low.at[slot], read_sem.at[slot, 1]),
        )

    HALF = R // 2
    width = min(512, HALF)

    def build(n, pieces):
        turned[...] = features(fall[n], False).T
        for half, (high_ref, low_ref) in enumerate(pieces):
            for c in range(HALF // width):
                at = slice(c * width, (c + 1) * width)
                whole = slice(half * HALF + c * width, half * HALF + (c + 1) * width)
                power = jnp.dot(turned[...], stat[:, whole], preferred_element_type=F32)
                value = jnp.exp2(power)
                high = value.astype(BF)
                high_ref[:, at] = high
                low_ref[:, at] = (value - high.astype(F32)).astype(F8)
                dacc[:, whole] += jnp.sum(value.reshape(B // 8, 8, width), axis=0)

    def build_group(g, _):
        for i in range(8):
            n = g * 8 + i
            if i % 2 == 0:
                o = g * 4 + i // 2

                @pl.when(o + 1 < NO)
                def _():
                    pass_on(o + 1, fall, f_recv, forward.at[0])
            else:
                arrived(fall.at[n], f_recv.at[n])
            if i in KEPT:
                at = g * len(KEPT) + KEPT.index(i)
                build(n, [(near_high.at[half, at], near_low.at[half, at]) for half in (0, 1)])
            else:
                h = g * len(SENT) + SENT.index(i)

                @pl.when(h >= STAGES // 2)
                def _():
                    for copy in writes(h - STAGES // 2, 0) + writes(h - STAGES // 2, 1):
                        copy.wait()

                slots = [lax.rem(2 * h + half, STAGES) for half in (0, 1)]
                build(n, [(stage_high.at[slot], stage_low.at[slot]) for slot in slots])
                for copy in writes(h, 0) + writes(h, 1):
                    copy.start()
        return 0

    lax.fori_loop(0, NB // 8, build_group, 0)

    for dz in range(Z):
        line_part[dz] = jnp.sum(dacc[:, dz * B : (dz + 1) * B], axis=0, keepdims=True)
    for dz in range(1, Z):
        push(line_part.at[dz], dgot.at[Z - dz], send.at[3], d_recv.at[Z - dz], along(dz))
    for h in range(NH - STAGES // 2, NH):
        for copy in writes(h, 0) + writes(h, 1):
            copy.wait()
    for t in range(STAGES):
        for copy in reads(t):
            copy.start()
    density = line_part[0]
    for dz in range(1, Z):
        arrived(dgot.at[dz], d_recv.at[dz])
        density = density + dgot[dz]
    iall[0] = 1.0 / (density * 2.0**-SHIFT)
    push(iall.at[0], iall.at[1], forward.at[2], i_recv.at[0], sibling)
    for o in range(1, NO):
        pass_on(o, sall, s_recv, forward.at[1])
    arrived(iall.at[1], i_recv.at[0])
    for o in range(1, NO):
        push(iall.at[pl.ds(0, 2)], iall.at[pl.ds(2 * o, 2)], send.at[4], i_recv.at[o], plane(o))
    acc[...] = jnp.zeros_like(acc)
    low_acc[...] = jnp.zeros_like(low_acc)
    gather_end(fall, send.at[0], forward.at[0])
    gather_end(sall, send.at[2], forward.at[1])
    left(zframes.at[pl.ds(0, Z - 1)], send.at[1])
    left(dgot.at[pl.ds(0, Z - 1)], send.at[3])
    for o in range(1, NO):
        arrived(iall.at[pl.ds(2 * o, 2)], i_recv.at[o])
    largest = jnp.max(jnp.max(iall[...], axis=0), axis=1, keepdims=True)
    low_weight = 400.0 / (6.0 * largest)

    def sweep(n, half, vectors, with_degree, high_ref, low_ref):
        inverse = iall[n]
        weights = vectors[n] * inverse
        high = weights.astype(BF)
        low = (weights - high.astype(F32)).astype(BF)
        rows = 2 * V
        pieces = [high, low]
        if with_degree:
            inverse_high = inverse.astype(BF).astype(F32)
            row = lax.broadcasted_iota(jnp.int32, (16, B), 0)
            pieces += [jnp.where(row < 8, inverse_high, inverse - inverse_high).astype(BF)]
            rows += 16
        spread = jnp.concatenate(pieces, axis=0)
        at = slice(half * HALF, (half + 1) * HALF)
        acc[0:rows, at] += jnp.dot(spread, high_ref[...], preferred_element_type=F32)
        low_acc[:, at] += jnp.dot((weights * low_weight).astype(F8), low_ref[...], preferred_element_type=F32)

    def sweep_half(half, vectors, recv, with_degree, passing, extra):
        early = half == 1

        def group(g, _):
            extra(g)
            for i in range(8):
                n = g * 8 + i
                if early and i % 2 == 1:
                    arrived(vectors.at[n], recv.at[n])
                elif early and passing:
                    o = g * 4 + i // 2

                    @pl.when(o + 1 < NO)
                    def _():
                        pass_on(o + 1, vectors, recv, forward.at[3])

                if i in KEPT:
                    at = g * len(KEPT) + KEPT.index(i)
                    sweep(n, half, vectors, with_degree, near_high.at[half, at], near_low.at[half, at])
                else:
                    t = (0 if early else NH) + g * len(SENT) + SENT.index(i)
                    for copy in reads(t):
                        copy.wait()
                    slot = lax.rem(t, STAGES)
                    sweep(n, half, vectors, with_degree, stage_high.at[slot], stage_low.at[slot])

                    @pl.when(t + STAGES < 2 * NH)
                    def _():
                        for copy in reads(t + STAGES):
                            copy.start()

            return 0

        lax.fori_loop(0, NB // 8, group, 0)

    def own_sum(half, got, recv, sem, with_degree):
        for dz in reversed(range(half * Z // 2, (half + 1) * Z // 2)):
            at = slice(dz * B, (dz + 1) * B)
            part[dz] = (acc[0:V, at] + acc[V : 2 * V, at]) * 2.0**-SHIFT + low_acc[:, at] * (
                2.0**-SHIFT / low_weight
            )
            if dz:
                push(part.at[dz], got.at[Z - dz], sem, recv.at[Z - dz], along(dz))
            if with_degree:
                line_part[dz] = (acc[2 * V : 2 * V + 1, at] + acc[2 * V + 8 : 2 * V + 9, at]) * 2.0**-SHIFT
                if dz:
                    push(line_part.at[dz], line_got.at[Z - dz], send.at[3], line_recv.at[Z - dz], along(dz))

    def own_total(source, got, recv):
        result = source[0]
        for dz in range(1, Z):
            arrived(got.at[dz], recv.at[dz])
            result = result + got[dz]
        return result

    def sweep_all(vectors, got, recv, v_recv, sem, with_degree, passing, extra):
        for half in (1, 0):
            sweep_half(half, vectors, v_recv, with_degree, passing, extra if half == 0 else lambda g: None)
            own_sum(half, got, recv, sem, with_degree)

    def gram_of(vectors):
        return lax.dot_general(
            vectors, vectors, (((1,), (1,)), ((), ())), precision=lax.Precision.HIGHEST, preferred_element_type=F32
        ) * (1.0 / total)

    def gram_send(which, vectors):
        gram_all[which, 0] = gram_of(vectors)
        for o in range(1, NO):
            push(gram_all.at[which, 0], gram_all.at[which, o], send.at[5 + which], p_recv.at[which, o], plane(o))

    def gram_turn(which):
        for o in range(1, NO):
            arrived(gram_all.at[which, o], p_recv.at[which, o])
        gram_col[which, 0] = jnp.sum(gram_all[which], axis=0)
        for d in range(1, 2 * Z):
            push(gram_col.at[which, 0], gram_col.at[which, d], send.at[7 + which], q_recv.at[which, d], post(d))

    def gram_total(which):
        for d in range(1, 2 * Z):
            arrived(gram_col.at[which, d], q_recv.at[which, d])
        return jnp.sum(gram_col[which], axis=0)

    def gram_end(which):
        left(gram_all.at[which, pl.ds(0, NO - 1)], send.at[5 + which])
        left(gram_col.at[which, pl.ds(0, 2 * Z - 1)], send.at[7 + which])

    sweep_all(sall, got_one, one_recv, s_recv, send.at[9], True, False, lambda g: None)
    for t in range(STAGES):
        for copy in reads(t):
            copy.start()
    acc[...] = jnp.zeros_like(acc)
    low_acc[...] = jnp.zeros_like(low_acc)
    left(iall.at[0], forward.at[2])
    left(iall.at[pl.ds(0, 2 * (NO - 1))], send.at[4])
    grown = own_total(part, got_one, one_recv)
    degree[...] = own_total(line_part, line_got, line_recv)
    grown = grown / degree[...]
    gall[0] = grown
    gather_start(gall.at[0], gall, g_recv, send.at[10], forward.at[3])
    gram_send(0, grown)
    left(part.at[pl.ds(0, Z - 1)], send.at[9])
    left(line_part.at[pl.ds(0, Z - 1)], send.at[3])

    def turn_first(g):
        @pl.when(g == NB // 8 - 1)
        def _():
            gram_turn(0)

    sweep_all(gall, got_two, two_recv, g_recv, send.at[11], False, True, turn_first)
    first = inverse_factor(gram_total(0))
    grown_two = own_total(part, got_two, two_recv) / degree[...]
    grown_two = jnp.dot(first, grown_two, precision=lax.Precision.HIGHEST, preferred_element_type=F32)
    gram_send(1, grown_two)
    gather_end(gall, send.at[10], forward.at[3])
    left(part.at[pl.ds(0, Z - 1)], send.at[11])
    gram_end(0)
    gram_turn(1)
    second = inverse_factor(gram_total(1))
    out[...] = jnp.dot(second, grown_two, precision=lax.Precision.HIGHEST, preferred_element_type=F32)
    gram_end(1)


def solution(mesh):
    X = math.isqrt(mesh.shape["row"] // 2)
    Z = mesh.shape["col"]
    NO, NB = X * X, 2 * X * X

    def step(frames, start):
        F, B = frames.shape
        V = start.shape[0]
        R = Z * B
        near, far = len(KEPT) * (NB // 8), len(SENT) * (NB // 8)
        vmem = pl.BlockSpec(memory_space=pltpu.VMEM)
        hbm = pl.BlockSpec(memory_space=pltpu.HBM)
        dma = pltpu.SemaphoreType.DMA
        basis, _, _ = pl.pallas_call(
            lambda *refs: kernel(X, Z, *refs),
            out_shape=(
                jax.ShapeDtypeStruct((V, B), F32),
                jax.ShapeDtypeStruct((2 * far, B, R // 2), BF),
                jax.ShapeDtypeStruct((2 * far, B, R // 2), F8),
            ),
            in_specs=[vmem, vmem],
            out_specs=(vmem, hbm, hbm),
            scratch_shapes=[
                pltpu.VMEM((2, near, B, R // 2), BF),
                pltpu.VMEM((2, near, B, R // 2), F8),
                pltpu.VMEM((STAGES, B, R // 2), BF),
                pltpu.VMEM((STAGES, B, R // 2), F8),
                pltpu.VMEM((Z, F, B), F32),
                pltpu.VMEM((NB, F, B), F32),
                pltpu.VMEM((NB, V, B), F32),
                pltpu.VMEM((NB, V, B), F32),
                pltpu.VMEM((NB, 1, B), F32),
                pltpu.VMEM((256, R), BF),
                pltpu.VMEM((B, 256), BF),
                pltpu.VMEM((2 * V + 16, R), F32),
                pltpu.VMEM((V, R), F32),
                pltpu.VMEM((8, R), F32),
                pltpu.VMEM((Z, V, B), F32),
                pltpu.VMEM((Z, 1, B), F32),
                pltpu.VMEM((Z, 1, B), F32),
                pltpu.VMEM((Z, 1, B), F32),
                pltpu.VMEM((Z, V, B), F32),
                pltpu.VMEM((Z, V, B), F32),
                pltpu.VMEM((1, B), F32),
                pltpu.VMEM((2, NO, V, V), F32),
                pltpu.VMEM((2, 2 * Z, V, V), F32),
                dma((NB,)), dma((NB,)), dma((NB,)),
                dma((Z,)), dma((Z,)), dma((Z,)), dma((NO,)), dma((Z,)), dma((Z,)),
                dma((2, NO)), dma((2, 2 * Z)),
                dma((12,)), dma((4,)), dma((STAGES, 2)), dma((STAGES, 2)),
            ],
            compiler_params=pltpu.CompilerParams(
                collective_id=0, has_side_effects=True, vmem_limit_bytes=64 * 1024 * 1024 - 512 * 1024
            ),
            name="diffusion",
        )(frames, start)
        return basis

    return jax.shard_map(
        step,
        mesh=mesh,
        in_specs=(P(None, ("row", "col")), P(None, ("row", "col"))),
        out_specs=P(None, ("row", "col")),
        check_vma=False,
    )
```

```python
import math

import jax
import jax.numpy as jnp
from jax import lax
from jax.experimental import pallas as pl
from jax.experimental.pallas import tpu as pltpu
from jax.sharding import PartitionSpec as P

MESH = pl.DeviceIdType.MESH
BF = jnp.bfloat16
F8 = jnp.float8_e4m3fn
F32 = jnp.float32
SHIFT = 17
BLOCKS = 3
FRAMES_AHEAD = 6
GROWN_AHEAD = 8
KEPT = (2, 4, 6)
SENT = (0, 1, 3, 5, 7)


def features(points, stationary):
    scaled = points * math.sqrt(math.log2(math.e) / 16.0 * (64.0 / points.shape[0]))
    high = scaled.astype(BF)
    low = (scaled - high.astype(F32)).astype(BF)
    half = 0.5 * jnp.sum(scaled * scaled, axis=0, keepdims=True)
    half = SHIFT - half if stationary else half
    one = half.astype(BF).astype(F32)
    two = (half - one).astype(BF).astype(F32)
    three = half - one - two
    row = lax.broadcasted_iota(jnp.int32, (16, points.shape[1]), 0)
    unit = jnp.ones_like(one)
    if stationary:
        first, rest, middle = (one, two, three), (-unit, -unit, -unit), (high, high, low)
    else:
        first, rest, middle = (unit, unit, unit), (one, two, three), (high, low, high)
    extra = jnp.zeros((16, points.shape[1]), F32)
    for index, value in enumerate(first + rest):
        extra = jnp.where(row == index, value, extra)
    pad = jnp.zeros((48, points.shape[1]), BF)
    return jnp.concatenate(middle + (extra.astype(BF), pad), axis=0)


def inverse_factor(gram):
    n = gram.shape[0]
    row = lax.broadcasted_iota(jnp.int32, (n, n), 0)
    column = lax.broadcasted_iota(jnp.int32, (n, n), 1)
    inverse = jnp.where(row == column, 1.0, 0.0).astype(F32)
    for c in range(n):
        pivot = gram[c : c + 1, c : c + 1]
        root = lax.rsqrt(pivot)
        root = root * (1.5 - 0.5 * pivot * root * root)
        line = gram[c : c + 1, :] * root
        line_inverse = inverse[c : c + 1, :] * root
        factor = jnp.where(row[:, :1] > c, gram[:, c : c + 1] * root, 0.0)
        gram = jnp.where(row == c, line, gram - factor * line)
        inverse = jnp.where(row == c, line_inverse, inverse - factor * line_inverse)
    return inverse


def chip_order(X):
    hops = [min(d, X - d) for d in range(X)]

    def key(place):
        return max(hops[place[0]], hops[place[1]]), hops[place[0]] + hops[place[1]], sum(place), place

    return sorted(((dx, dy) for dx in range(X) for dy in range(X)), key=key)


def kernel(
    X, Z, frames, start, out, far_high, far_low,
    near_high, near_low, stage_high, stage_low, zframes, fall, sall, gall, iall, stat, turned,
    acc, low_acc, dacc, part, line_part, dgot, line_got, got_one, got_two, degree, gram_all, gram_col,
    f_recv, s_recv, g_recv, zf_recv, d_recv, line_recv, i_recv, one_recv, two_recv, p_recv, q_recv,
    send, forward, write_sem, read_sem,
):
    NO = X * X
    NB = 2 * NO
    B = frames.shape[1]
    R = Z * B
    V = start.shape[0]
    NH = len(SENT) * (NB // 8)
    total = X * X * 2 * Z * B
    me, z = lax.axis_index("row"), lax.axis_index("col")
    core, chip = lax.rem(me, 2), me // 2
    cx, cy = chip // X, lax.rem(chip, X)

    rows_x = [lax.rem(cx + d, X) * (2 * X) + core for d in range(X)]
    rows_y = [lax.rem(cy + d, X) * 2 for d in range(X)]

    places = chip_order(X)

    def plane(o):
        dx, dy = places[o]
        return {"row": rows_x[(X - dx) % X] + rows_y[(X - dy) % X], "col": z}

    sibling = {"row": chip * 2 + 1 - core, "col": z}

    cols = [lax.rem(z + d, Z) for d in range(Z)]

    def along(dz):
        return {"row": me, "col": cols[dz]}

    def post(d):
        return {"row": me if d < Z else chip * 2 + 1 - core, "col": cols[(Z - d % Z) % Z]}

    def push(src, dst, send_sem, recv_sem, device):
        pltpu.make_async_remote_copy(
            src_ref=src, dst_ref=dst, send_sem=send_sem, recv_sem=recv_sem, device_id=device, device_id_type=MESH
        ).start()

    def arrived(ref, sem):
        pltpu.make_async_remote_copy(
            src_ref=ref, dst_ref=ref, send_sem=send.at[0], recv_sem=sem, device_id=sibling, device_id_type=MESH
        ).wait_recv()

    def left(ref, sem):
        pltpu.make_async_remote_copy(
            src_ref=ref, dst_ref=ref, send_sem=sem, recv_sem=f_recv.at[0], device_id=sibling, device_id_type=MESH
        ).wait_send()

    def gather_send(o, mine, buffer, recv, sem):
        if 0 < o < NO:
            push(mine, buffer.at[2 * o], sem, recv.at[2 * o], plane(o))

    def gather_start(ahead, mine, buffer, recv, sem, forward_sem):
        push(mine, buffer.at[1], forward_sem, recv.at[1], sibling)
        for o in range(1, ahead):
            gather_send(o, mine, buffer, recv, sem)

    def beside(g, step, send_some):
        for known in range(NB // 8):

            @pl.when(g == known)
            def _(known=known):
                send_some(known * 4 + step)

    def pass_on(o, buffer, recv, forward_sem):
        arrived(buffer.at[2 * o], recv.at[2 * o])
        push(buffer.at[2 * o], buffer.at[2 * o + 1], forward_sem, recv.at[2 * o + 1], sibling)

    def gather_end(buffer, sem, forward_sem):
        left(buffer.at[pl.ds(0, NO - 1)], sem)
        left(buffer.at[pl.ds(0, NO)], forward_sem)

    barrier = pltpu.get_barrier_semaphore()

    for o in range(1, NO):
        pl.semaphore_signal(barrier, inc=1, device_id=plane(o), device_id_type=MESH)
    for d in range(1, 2 * Z):
        pl.semaphore_signal(barrier, inc=1, device_id=post(d), device_id_type=MESH)
    pl.semaphore_wait(barrier, NO - 1 + 2 * Z - 1)

    for dz in range(1, Z):
        push(frames, zframes.at[Z - dz], send.at[1], zf_recv.at[Z - dz], along(dz))
    gather_start(FRAMES_AHEAD, frames, fall, f_recv, send.at[0], forward.at[0])
    gather_start(0, start, sall, s_recv, send.at[2], forward.at[1])
    fall[0] = frames[...]
    sall[0] = start[...]
    dacc[...] = jnp.zeros_like(dacc)
    stat[:, 0:B] = features(frames[...], True)
    for dz in range(1, Z):
        arrived(zframes.at[dz], zf_recv.at[dz])
        stat[:, dz * B : (dz + 1) * B] = features(zframes[dz], True)

    STAGES = BLOCKS * Z

    def writes(h):
        copies = []
        for dz in range(Z):
            slot = lax.rem(Z * h + dz, STAGES)
            copies += [
                pltpu.make_async_copy(stage_high.at[slot], far_high.at[dz * NH + h], write_sem.at[slot, 0]),
                pltpu.make_async_copy(stage_low.at[slot], far_low.at[dz * NH + h], write_sem.at[slot, 1]),
            ]
        return copies

    def reads(t, at):
        slot = lax.rem(t, STAGES)
        return (
            pltpu.make_async_copy(far_high.at[at], stage_high.at[slot], read_sem.at[slot, 0]),
            pltpu.make_async_copy(far_low.at[at], stage_low.at[slot], read_sem.at[slot, 1]),
        )

    def read_start(t):
        @pl.when(t < (Z - 1) * NH)
        def _():
            for copy in reads(t, (1 + lax.rem(t, Z - 1)) * NH + t // (Z - 1)):
                copy.start()

        @pl.when((t >= (Z - 1) * NH) & (t < Z * NH))
        def _():
            for copy in reads(t, t - (Z - 1) * NH):
                copy.start()

    def build(n, pieces):
        turned[...] = features(fall[n], False).T
        for dz, (high_ref, low_ref) in enumerate(pieces):
            at = slice(dz * B, (dz + 1) * B)
            power = jnp.dot(turned[...], stat[:, at], preferred_element_type=F32)
            value = jnp.exp2(power)
            high = value.astype(BF)
            high_ref[...] = high
            low_ref[...] = (value - high.astype(F32)).astype(F8)
            dacc[:, at] += jnp.sum(value.reshape(B // 8, 8, B), axis=0)

    def send_inputs(o):
        gather_send(o + FRAMES_AHEAD, frames, fall, f_recv, send.at[0])
        later = 2 * (o - NO // 2)
        gather_send(later + 1, start, sall, s_recv, send.at[2])
        gather_send(later + 2, start, sall, s_recv, send.at[2])

    def build_group(g, _):
        for i in range(8):
            n = g * 8 + i
            if i % 2 == 0:
                beside(g, i // 2, send_inputs)
                o = g * 4 + i // 2

                @pl.when(o + 1 < NO)
                def _():
                    pass_on(o + 1, fall, f_recv, forward.at[0])
            else:
                arrived(fall.at[n], f_recv.at[n])
            if i in KEPT:
                at = g * len(KEPT) + KEPT.index(i)
                build(n, [(near_high.at[dz, at], near_low.at[dz, at]) for dz in range(Z)])
            else:
                h = g * len(SENT) + SENT.index(i)

                @pl.when(h >= BLOCKS)
                def _():
                    for copy in writes(h - BLOCKS):
                        copy.wait()

                slots = [lax.rem(Z * h + dz, STAGES) for dz in range(Z)]
                build(n, [(stage_high.at[slot], stage_low.at[slot]) for slot in slots])
                for copy in writes(h):
                    copy.start()
        return 0

    lax.fori_loop(0, NB // 8, build_group, 0)

    for dz in range(Z):
        line_part[dz] = jnp.sum(dacc[:, dz * B : (dz + 1) * B], axis=0, keepdims=True)
    for dz in range(Z):
        for other in range(2):
            if dz or other:
                place = {"row": sibling["row"] if other else me, "col": cols[dz]}
                slot = (Z - dz) % Z
                push(line_part.at[dz], dgot.at[other, slot], send.at[3], d_recv.at[other, slot], place)
    for h in range(NH - BLOCKS, NH):
        for copy in writes(h):
            copy.wait()
    for t in range(STAGES):
        read_start(t)
    for o in range(1, NO):
        pass_on(o, sall, s_recv, forward.at[1])
    dgot[0, 0] = line_part[0]
    for other in range(2):
        for dz in range(Z):
            if dz or other:
                arrived(dgot.at[other, dz], d_recv.at[other, dz])
        density = sum(dgot[other, dz] for dz in range(Z))
        iall[other] = 1.0 / (density * 2.0**-SHIFT)
    for o in range(1, NO):
        push(iall.at[pl.ds(0, 2)], iall.at[pl.ds(2 * o, 2)], send.at[4], i_recv.at[o], plane(o))
    acc[...] = jnp.zeros_like(acc)
    low_acc[...] = jnp.zeros_like(low_acc)
    gather_end(fall, send.at[0], forward.at[0])
    gather_end(sall, send.at[2], forward.at[1])
    left(zframes.at[pl.ds(0, Z - 1)], send.at[1])
    left(iall.at[pl.ds(0, 2 * Z - 1)], send.at[3])
    for o in range(1, NO):
        arrived(iall.at[pl.ds(2 * o, 2)], i_recv.at[o])
    largest = jnp.max(jnp.max(iall[...], axis=0), axis=1, keepdims=True)
    low_weight = 400.0 / (6.0 * largest)

    def sweep(n, vectors, with_degree, pieces):
        inverse = iall[n]
        weights = vectors[n] * inverse
        high = weights.astype(BF)
        low = (weights - high.astype(F32)).astype(BF)
        rows = 2 * V
        spread = [high, low]
        if with_degree:
            inverse_high = inverse.astype(BF).astype(F32)
            row = lax.broadcasted_iota(jnp.int32, (16, B), 0)
            spread += [jnp.where(row < 8, inverse_high, inverse - inverse_high).astype(BF)]
            rows += 16
        spread = jnp.concatenate(spread, axis=0)
        coarse = (weights * low_weight).astype(F8)
        for dz, high_ref, low_ref in pieces:
            at = slice(dz * B, (dz + 1) * B)
            acc[0:rows, at] += jnp.dot(spread, high_ref[...], preferred_element_type=F32)
            low_acc[:, at] += jnp.dot(coarse, low_ref[...], preferred_element_type=F32)

    def send_grown(o):
        gather_send(o + GROWN_AHEAD, gall.at[0], gall, g_recv, send.at[10])

    def sweep_part(first, pieces, vectors, recv, with_degree, passing, extra):
        def group(g, _):
            extra(g)
            for i in range(8):
                n = g * 8 + i
                if first and i % 2 == 1:
                    arrived(vectors.at[n], recv.at[n])
                elif first and passing:
                    o = g * 4 + i // 2
                    beside(g, i // 2, send_grown)

                    @pl.when(o + 1 < NO)
                    def _():
                        pass_on(o + 1, vectors, recv, forward.at[3])

                if i in KEPT:
                    at = g * len(KEPT) + KEPT.index(i)
                    sweep(n, vectors, with_degree, [(dz, near_high.at[dz, at], near_low.at[dz, at]) for dz in pieces])
                else:
                    h = g * len(SENT) + SENT.index(i)
                    times = [(Z - 1) * h + k if first else (Z - 1) * NH + h for k in range(len(pieces))]
                    taken = []
                    for t, dz in zip(times, pieces):
                        for copy in reads(t, dz * NH + h):
                            copy.wait()
                        slot = lax.rem(t, STAGES)
                        taken.append((dz, stage_high.at[slot], stage_low.at[slot]))
                    sweep(n, vectors, with_degree, taken)
                    for t in times:
                        read_start(t + STAGES)

            return 0

        lax.fori_loop(0, NB // 8, group, 0)

    def own_sum(dz, got, recv, sem, with_degree):
        at = slice(dz * B, (dz + 1) * B)
        part[dz] = (acc[0:V, at] + acc[V : 2 * V, at]) * 2.0**-SHIFT + low_acc[:, at] * (2.0**-SHIFT / low_weight)
        if dz:
            push(part.at[dz], got.at[Z - dz], sem, recv.at[Z - dz], along(dz))
        if with_degree:
            line_part[dz] = (acc[2 * V : 2 * V + 1, at] + acc[2 * V + 8 : 2 * V + 9, at]) * 2.0**-SHIFT
            if dz:
                push(line_part.at[dz], line_got.at[Z - dz], send.at[3], line_recv.at[Z - dz], along(dz))

    def own_total(source, got, recv):
        result = source[0]
        for dz in range(1, Z):
            arrived(got.at[dz], recv.at[dz])
            result = result + got[dz]
        return result

    def sweep_all(vectors, got, recv, v_recv, sem, with_degree, passing, extra):
        for first, pieces in ((True, range(1, Z)), (False, range(1))):
            sweep_part(first, pieces, vectors, v_recv, with_degree, passing, (lambda g: None) if first else extra)
            for dz in pieces:
                own_sum(dz, got, recv, sem, with_degree)

    def gram_of(vectors):
        return lax.dot_general(
            vectors, vectors, (((1,), (1,)), ((), ())), precision=lax.Precision.HIGHEST, preferred_element_type=F32
        ) * (1.0 / total)

    def gram_send(which, vectors):
        gram = gram_of(vectors)
        gram_all[which, 0] = jnp.concatenate([gram[i : i + 8] for i in range(0, V, 8)], axis=1)
        for o in range(1, NO):
            push(gram_all.at[which, 0], gram_all.at[which, o], send.at[5 + which], p_recv.at[which, o], plane(o))

    def gram_turn(which):
        for o in range(1, NO):
            arrived(gram_all.at[which, o], p_recv.at[which, o])
        gram_col[which, 0] = jnp.sum(gram_all[which], axis=0)
        for d in range(1, 2 * Z):
            push(gram_col.at[which, 0], gram_col.at[which, d], send.at[7 + which], q_recv.at[which, d], post(d))

    def gram_total(which):
        for d in range(1, 2 * Z):
            arrived(gram_col.at[which, d], q_recv.at[which, d])
        packed = jnp.sum(gram_col[which], axis=0)
        return jnp.concatenate([packed[:, i : i + V] for i in range(0, V * (V // 8), V)], axis=0)

    def gram_end(which):
        left(gram_all.at[which, pl.ds(0, NO - 1)], send.at[5 + which])
        left(gram_col.at[which, pl.ds(0, 2 * Z - 1)], send.at[7 + which])

    sweep_all(sall, got_one, one_recv, s_recv, send.at[9], True, False, lambda g: None)
    for t in range(STAGES):
        read_start(t)
    acc[...] = jnp.zeros_like(acc)
    low_acc[...] = jnp.zeros_like(low_acc)
    left(iall.at[pl.ds(0, 2 * (NO - 1))], send.at[4])
    grown = own_total(part, got_one, one_recv)
    degree[...] = own_total(line_part, line_got, line_recv)
    grown = grown / degree[...]
    gall[0] = grown
    gather_start(GROWN_AHEAD, gall.at[0], gall, g_recv, send.at[10], forward.at[3])
    gram_send(0, grown)
    left(part.at[pl.ds(0, Z - 1)], send.at[9])
    left(line_part.at[pl.ds(0, Z - 1)], send.at[3])

    def turn_first(g):
        @pl.when(g == NB // 8 - 1)
        def _():
            gram_turn(0)

    sweep_all(gall, got_two, two_recv, g_recv, send.at[11], False, True, turn_first)
    first = inverse_factor(gram_total(0))
    grown_two = own_total(part, got_two, two_recv) / degree[...]
    grown_two = jnp.dot(first, grown_two, precision=lax.Precision.HIGHEST, preferred_element_type=F32)
    gram_send(1, grown_two)
    gather_end(gall, send.at[10], forward.at[3])
    left(part.at[pl.ds(0, Z - 1)], send.at[11])
    gram_end(0)
    gram_turn(1)
    second = inverse_factor(gram_total(1))
    out[...] = jnp.dot(second, grown_two, precision=lax.Precision.HIGHEST, preferred_element_type=F32)
    gram_end(1)


def solution(mesh):
    X = math.isqrt(mesh.shape["row"] // 2)
    Z = mesh.shape["col"]
    NO, NB = X * X, 2 * X * X

    def step(frames, start):
        F, B = frames.shape
        V = start.shape[0]
        R = Z * B
        near, far = len(KEPT) * (NB // 8), len(SENT) * (NB // 8)
        vmem = pl.BlockSpec(memory_space=pltpu.VMEM)
        hbm = pl.BlockSpec(memory_space=pltpu.HBM)
        dma = pltpu.SemaphoreType.DMA
        basis, _, _ = pl.pallas_call(
            lambda *refs: kernel(X, Z, *refs),
            out_shape=(
                jax.ShapeDtypeStruct((V, B), F32),
                jax.ShapeDtypeStruct((Z * far, B, B), BF),
                jax.ShapeDtypeStruct((Z * far, B, B), F8),
            ),
            in_specs=[vmem, vmem],
            out_specs=(vmem, hbm, hbm),
            scratch_shapes=[
                pltpu.VMEM((Z, near, B, B), BF),
                pltpu.VMEM((Z, near, B, B), F8),
                pltpu.VMEM((BLOCKS * Z, B, B), BF),
                pltpu.VMEM((BLOCKS * Z, B, B), F8),
                pltpu.VMEM((Z, F, B), F32),
                pltpu.VMEM((NB, F, B), F32),
                pltpu.VMEM((NB, V, B), F32),
                pltpu.VMEM((NB, V, B), F32),
                pltpu.VMEM((NB, 1, B), F32),
                pltpu.VMEM((256, R), BF),
                pltpu.VMEM((B, 256), BF),
                pltpu.VMEM((2 * V + 16, R), F32),
                pltpu.VMEM((V, R), F32),
                pltpu.VMEM((8, R), F32),
                pltpu.VMEM((Z, V, B), F32),
                pltpu.VMEM((Z, 1, B), F32),
                pltpu.VMEM((2, Z, 1, B), F32),
                pltpu.VMEM((Z, 1, B), F32),
                pltpu.VMEM((Z, V, B), F32),
                pltpu.VMEM((Z, V, B), F32),
                pltpu.VMEM((1, B), F32),
                pltpu.VMEM((2, NO, 8, V * V // 8), F32),
                pltpu.VMEM((2, 2 * Z, 8, V * V // 8), F32),
                dma((NB,)), dma((NB,)), dma((NB,)),
                dma((Z,)), dma((2, Z)), dma((Z,)), dma((NO,)), dma((Z,)), dma((Z,)),
                dma((2, NO)), dma((2, 2 * Z)),
                dma((12,)), dma((4,)), dma((BLOCKS * Z, 2)), dma((BLOCKS * Z, 2)),
            ],
            compiler_params=pltpu.CompilerParams(
                collective_id=0, has_side_effects=True, vmem_limit_bytes=64 * 1024 * 1024 - 512 * 1024
            ),
            name="diffusion",
        )(frames, start)
        return basis

    return jax.shard_map(
        step,
        mesh=mesh,
        in_specs=(P(None, ("row", "col")), P(None, ("row", "col"))),
        out_specs=P(None, ("row", "col")),
        check_vma=False,
    )
```

```python
import math

import jax
import jax.numpy as jnp
from jax import lax
from jax.experimental import pallas as pl
from jax.experimental.pallas import tpu as pltpu
from jax.sharding import PartitionSpec as P

MESH = pl.DeviceIdType.MESH
BF = jnp.bfloat16
F8 = jnp.float8_e4m3fn
F32 = jnp.float32
SHIFT = 17
BLOCKS = 3
FRAMES_AHEAD = 5
FRAMES_RAMP = 2
GROWN_AHEAD = 8
KEPT = (2, 4, 6)
SENT = (0, 1, 3, 5, 7)


def features(points, stationary):
    scaled = points * math.sqrt(math.log2(math.e) / 16.0 * (64.0 / points.shape[0]))
    high = scaled.astype(BF)
    low = (scaled - high.astype(F32)).astype(BF)
    half = 0.5 * jnp.sum(scaled * scaled, axis=0, keepdims=True)
    half = SHIFT - half if stationary else half
    one = half.astype(BF).astype(F32)
    two = (half - one).astype(BF).astype(F32)
    three = half - one - two
    row = lax.broadcasted_iota(jnp.int32, (16, points.shape[1]), 0)
    unit = jnp.ones_like(one)
    if stationary:
        first, rest, middle = (one, two, three), (-unit, -unit, -unit), (high, high, low)
    else:
        first, rest, middle = (unit, unit, unit), (one, two, three), (high, low, high)
    extra = jnp.zeros((16, points.shape[1]), F32)
    for index, value in enumerate(first + rest):
        extra = jnp.where(row == index, value, extra)
    pad = jnp.zeros((48, points.shape[1]), BF)
    return jnp.concatenate(middle + (extra.astype(BF), pad), axis=0)


def inverse_factor(gram):
    n = gram.shape[0]
    row = lax.broadcasted_iota(jnp.int32, (n, n), 0)
    column = lax.broadcasted_iota(jnp.int32, (n, n), 1)
    inverse = jnp.where(row == column, 1.0, 0.0).astype(F32)
    for c in range(n):
        pivot = gram[c : c + 1, c : c + 1]
        root = lax.rsqrt(pivot)
        root = root * (1.5 - 0.5 * pivot * root * root)
        line = gram[c : c + 1, :] * root
        line_inverse = inverse[c : c + 1, :] * root
        factor = jnp.where(row[:, :1] > c, gram[:, c : c + 1] * root, 0.0)
        gram = jnp.where(row == c, line, gram - factor * line)
        inverse = jnp.where(row == c, line_inverse, inverse - factor * line_inverse)
    return inverse


def chip_order(X):
    hops = [min(d, X - d) for d in range(X)]

    def key(place):
        return max(hops[place[0]], hops[place[1]]), hops[place[0]] + hops[place[1]], sum(place), place

    return sorted(((dx, dy) for dx in range(X) for dy in range(X)), key=key)


def kernel(
    X, Z, frames, start, out, far_high, far_low,
    near_high, near_low, stage_high, stage_low, zframes, fall, sall, gall, iall, stat, turned,
    acc, low_acc, dacc, part, line_part, dgot, line_got, got_one, got_two, degree, gram_all, gram_col,
    f_recv, s_recv, g_recv, zf_recv, d_recv, line_recv, i_recv, one_recv, two_recv, p_recv, q_recv,
    send, forward, write_sem, read_sem,
):
    NO = X * X
    NB = 2 * NO
    B = frames.shape[1]
    R = Z * B
    V = start.shape[0]
    NH = len(SENT) * (NB // 8)
    total = X * X * 2 * Z * B
    me, z = lax.axis_index("row"), lax.axis_index("col")
    core, chip = lax.rem(me, 2), me // 2
    cx, cy = chip // X, lax.rem(chip, X)

    rows_x = [lax.rem(cx + d, X) * (2 * X) + core for d in range(X)]
    rows_y = [lax.rem(cy + d, X) * 2 for d in range(X)]

    places = chip_order(X)

    def plane(o):
        dx, dy = places[o]
        return {"row": rows_x[(X - dx) % X] + rows_y[(X - dy) % X], "col": z}

    sibling = {"row": chip * 2 + 1 - core, "col": z}

    cols = [lax.rem(z + d, Z) for d in range(Z)]

    def along(dz):
        return {"row": me, "col": cols[dz]}

    def post(d):
        return {"row": me if d < Z else chip * 2 + 1 - core, "col": cols[(Z - d % Z) % Z]}

    def push(src, dst, send_sem, recv_sem, device):
        pltpu.make_async_remote_copy(
            src_ref=src, dst_ref=dst, send_sem=send_sem, recv_sem=recv_sem, device_id=device, device_id_type=MESH
        ).start()

    def arrived(ref, sem):
        pltpu.make_async_remote_copy(
            src_ref=ref, dst_ref=ref, send_sem=send.at[0], recv_sem=sem, device_id=sibling, device_id_type=MESH
        ).wait_recv()

    def left(ref, sem):
        pltpu.make_async_remote_copy(
            src_ref=ref, dst_ref=ref, send_sem=sem, recv_sem=f_recv.at[0], device_id=sibling, device_id_type=MESH
        ).wait_send()

    def gather_send(o, mine, buffer, recv, sem):
        if 0 < o < NO:
            push(mine, buffer.at[2 * o], sem, recv.at[2 * o], plane(o))

    def gather_start(ahead, mine, buffer, recv, sem, forward_sem):
        push(mine, buffer.at[1], forward_sem, recv.at[1], sibling)
        for o in range(1, ahead):
            gather_send(o, mine, buffer, recv, sem)

    def beside(g, step, send_some):
        for known in range(NB // 8):

            @pl.when(g == known)
            def _(known=known):
                send_some(known * 4 + step)

    def pass_on(o, buffer, recv, forward_sem):
        arrived(buffer.at[2 * o], recv.at[2 * o])
        push(buffer.at[2 * o], buffer.at[2 * o + 1], forward_sem, recv.at[2 * o + 1], sibling)

    def gather_end(buffer, sem, forward_sem):
        left(buffer.at[pl.ds(0, NO - 1)], sem)
        left(buffer.at[pl.ds(0, NO)], forward_sem)

    barrier = pltpu.get_barrier_semaphore()

    for o in range(1, NO):
        pl.semaphore_signal(barrier, inc=1, device_id=plane(o), device_id_type=MESH)
    for d in range(1, 2 * Z):
        pl.semaphore_signal(barrier, inc=1, device_id=post(d), device_id_type=MESH)
    fall[0] = frames[...]
    sall[0] = start[...]
    dacc[...] = jnp.zeros_like(dacc)
    stat[:, 0:B] = features(frames[...], True)
    pl.semaphore_wait(barrier, NO - 1 + 2 * Z - 1)

    for dz in range(1, Z):
        push(frames, zframes.at[Z - dz], send.at[1], zf_recv.at[Z - dz], along(dz))
    gather_start(FRAMES_AHEAD, frames, fall, f_recv, send.at[0], forward.at[0])
    gather_start(0, start, sall, s_recv, send.at[2], forward.at[1])
    for dz in range(1, Z):
        arrived(zframes.at[dz], zf_recv.at[dz])
        stat[:, dz * B : (dz + 1) * B] = features(zframes[dz], True)

    STAGES = BLOCKS * Z

    def writes(h):
        copies = []
        for dz in range(Z):
            slot = lax.rem(Z * h + dz, STAGES)
            copies += [
                pltpu.make_async_copy(stage_high.at[slot], far_high.at[dz * NH + h], write_sem.at[slot, 0]),
                pltpu.make_async_copy(stage_low.at[slot], far_low.at[dz * NH + h], write_sem.at[slot, 1]),
            ]
        return copies

    def reads(t, at):
        slot = lax.rem(t, STAGES)
        return (
            pltpu.make_async_copy(far_high.at[at], stage_high.at[slot], read_sem.at[slot, 0]),
            pltpu.make_async_copy(far_low.at[at], stage_low.at[slot], read_sem.at[slot, 1]),
        )

    def read_start(t):
        @pl.when(t < (Z - 1) * NH)
        def _():
            for copy in reads(t, (1 + lax.rem(t, Z - 1)) * NH + t // (Z - 1)):
                copy.start()

        @pl.when((t >= (Z - 1) * NH) & (t < Z * NH))
        def _():
            for copy in reads(t, t - (Z - 1) * NH):
                copy.start()

    def build(n, pieces):
        turned[...] = features(fall[n], False).T
        for dz, (high_ref, low_ref) in enumerate(pieces):
            at = slice(dz * B, (dz + 1) * B)
            power = jnp.dot(turned[...], stat[:, at], preferred_element_type=F32)
            value = jnp.exp2(power)
            high = value.astype(BF)
            high_ref[...] = high
            low_ref[...] = (value - high.astype(F32)).astype(F8)
            dacc[:, at] += jnp.sum(value.reshape(B // 8, 8, B), axis=0)

    def send_inputs(o):
        steps = (2 * o, 2 * o + 1) if o < FRAMES_RAMP else (o + FRAMES_RAMP,)
        for later in steps:
            gather_send(FRAMES_AHEAD + later, frames, fall, f_recv, send.at[0])
        later = 2 * (o - NO // 2)
        gather_send(later + 1, start, sall, s_recv, send.at[2])
        gather_send(later + 2, start, sall, s_recv, send.at[2])

    def build_group(g, _):
        for i in range(8):
            n = g * 8 + i
            if i % 2 == 0:
                beside(g, i // 2, send_inputs)
                o = g * 4 + i // 2

                @pl.when(o + 1 < NO)
                def _():
                    pass_on(o + 1, fall, f_recv, forward.at[0])
            else:
                arrived(fall.at[n], f_recv.at[n])
            if i in KEPT:
                at = g * len(KEPT) + KEPT.index(i)
                build(n, [(near_high.at[dz, at], near_low.at[dz, at]) for dz in range(Z)])
            else:
                h = g * len(SENT) + SENT.index(i)

                @pl.when(h >= BLOCKS)
                def _():
                    for copy in writes(h - BLOCKS):
                        copy.wait()

                slots = [lax.rem(Z * h + dz, STAGES) for dz in range(Z)]
                build(n, [(stage_high.at[slot], stage_low.at[slot]) for slot in slots])
                for copy in writes(h):
                    copy.start()
        return 0

    lax.fori_loop(0, NB // 8, build_group, 0)

    for dz in range(Z):
        line_part[dz] = jnp.sum(dacc[:, dz * B : (dz + 1) * B], axis=0, keepdims=True)
    for dz in range(Z):
        for other in range(2):
            if dz or other:
                place = {"row": sibling["row"] if other else me, "col": cols[dz]}
                slot = (Z - dz) % Z
                push(line_part.at[dz], dgot.at[other, slot], send.at[3], d_recv.at[other, slot], place)
    for h in range(NH - BLOCKS, NH):
        for copy in writes(h):
            copy.wait()
    for t in range(STAGES):
        read_start(t)
    for o in range(1, NO):
        pass_on(o, sall, s_recv, forward.at[1])
    dgot[0, 0] = line_part[0]
    for other in range(2):
        for dz in range(Z):
            if dz or other:
                arrived(dgot.at[other, dz], d_recv.at[other, dz])
        density = sum(dgot[other, dz] for dz in range(Z))
        iall[other] = 1.0 / (density * 2.0**-SHIFT)
    for o in range(1, NO):
        push(iall.at[pl.ds(0, 2)], iall.at[pl.ds(2 * o, 2)], send.at[4], i_recv.at[o], plane(o))
    acc[...] = jnp.zeros_like(acc)
    low_acc[...] = jnp.zeros_like(low_acc)
    gather_end(fall, send.at[0], forward.at[0])
    gather_end(sall, send.at[2], forward.at[1])
    left(zframes.at[pl.ds(0, Z - 1)], send.at[1])
    left(iall.at[pl.ds(0, 2 * Z - 1)], send.at[3])
    for o in range(1, NO):
        arrived(iall.at[pl.ds(2 * o, 2)], i_recv.at[o])
    largest = jnp.max(jnp.max(iall[...], axis=0), axis=1, keepdims=True)
    low_weight = 400.0 / (6.0 * largest)

    def sweep(n, vectors, with_degree, pieces):
        inverse = iall[n]
        weights = vectors[n] * inverse
        high = weights.astype(BF)
        low = (weights - high.astype(F32)).astype(BF)
        rows = 2 * V
        spread = [high, low]
        if with_degree:
            inverse_high = inverse.astype(BF).astype(F32)
            row = lax.broadcasted_iota(jnp.int32, (16, B), 0)
            spread += [jnp.where(row < 8, inverse_high, inverse - inverse_high).astype(BF)]
            rows += 16
        spread = jnp.concatenate(spread, axis=0)
        coarse = (weights * low_weight).astype(F8)
        for dz, high_ref, low_ref in pieces:
            at = slice(dz * B, (dz + 1) * B)
            acc[0:rows, at] += jnp.dot(spread, high_ref[...], preferred_element_type=F32)
            low_acc[:, at] += jnp.dot(coarse, low_ref[...], preferred_element_type=F32)

    def send_grown(o):
        gather_send(o + GROWN_AHEAD, gall.at[0], gall, g_recv, send.at[10])

    def sweep_part(first, pieces, vectors, recv, with_degree, passing, extra):
        def group(g, _):
            extra(g)
            for i in range(8):
                n = g * 8 + i
                if first and i % 2 == 1:
                    arrived(vectors.at[n], recv.at[n])
                elif first and passing:
                    o = g * 4 + i // 2
                    beside(g, i // 2, send_grown)

                    @pl.when(o + 1 < NO)
                    def _():
                        pass_on(o + 1, vectors, recv, forward.at[3])

                if i in KEPT:
                    at = g * len(KEPT) + KEPT.index(i)
                    sweep(n, vectors, with_degree, [(dz, near_high.at[dz, at], near_low.at[dz, at]) for dz in pieces])
                else:
                    h = g * len(SENT) + SENT.index(i)
                    times = [(Z - 1) * h + k if first else (Z - 1) * NH + h for k in range(len(pieces))]
                    taken = []
                    for t, dz in zip(times, pieces):
                        for copy in reads(t, dz * NH + h):
                            copy.wait()
                        slot = lax.rem(t, STAGES)
                        taken.append((dz, stage_high.at[slot], stage_low.at[slot]))
                    sweep(n, vectors, with_degree, taken)
                    for t in times:
                        read_start(t + STAGES)

            return 0

        lax.fori_loop(0, NB // 8, group, 0)

    def own_sum(dz, got, recv, sem, with_degree):
        at = slice(dz * B, (dz + 1) * B)
        part[dz] = (acc[0:V, at] + acc[V : 2 * V, at]) * 2.0**-SHIFT + low_acc[:, at] * (2.0**-SHIFT / low_weight)
        if dz:
            push(part.at[dz], got.at[Z - dz], sem, recv.at[Z - dz], along(dz))
        if with_degree:
            line_part[dz] = (acc[2 * V : 2 * V + 1, at] + acc[2 * V + 8 : 2 * V + 9, at]) * 2.0**-SHIFT
            if dz:
                push(line_part.at[dz], line_got.at[Z - dz], send.at[3], line_recv.at[Z - dz], along(dz))

    def own_total(source, got, recv):
        result = source[0]
        for dz in range(1, Z):
            arrived(got.at[dz], recv.at[dz])
            result = result + got[dz]
        return result

    def sweep_all(vectors, got, recv, v_recv, sem, with_degree, passing, extra):
        for first, pieces in ((True, range(1, Z)), (False, range(1))):
            sweep_part(first, pieces, vectors, v_recv, with_degree, passing, (lambda g: None) if first else extra)
            for dz in pieces:
                own_sum(dz, got, recv, sem, with_degree)

    def gram_of(vectors):
        return lax.dot_general(
            vectors, vectors, (((1,), (1,)), ((), ())), precision=lax.Precision.HIGHEST, preferred_element_type=F32
        ) * (1.0 / total)

    def gram_send(which, vectors):
        gram = gram_of(vectors)
        gram_all[which, 0] = jnp.concatenate([gram[i : i + 8] for i in range(0, V, 8)], axis=1)
        for o in range(1, NO):
            push(gram_all.at[which, 0], gram_all.at[which, o], send.at[5 + which], p_recv.at[which, o], plane(o))

    def gram_turn(which):
        for o in range(1, NO):
            arrived(gram_all.at[which, o], p_recv.at[which, o])
        gram_col[which, 0] = jnp.sum(gram_all[which], axis=0)
        for d in range(1, 2 * Z):
            push(gram_col.at[which, 0], gram_col.at[which, d], send.at[7 + which], q_recv.at[which, d], post(d))

    def gram_total(which):
        for d in range(1, 2 * Z):
            arrived(gram_col.at[which, d], q_recv.at[which, d])
        packed = jnp.sum(gram_col[which], axis=0)
        return jnp.concatenate([packed[:, i : i + V] for i in range(0, V * (V // 8), V)], axis=0)

    def gram_end(which):
        left(gram_all.at[which, pl.ds(0, NO - 1)], send.at[5 + which])
        left(gram_col.at[which, pl.ds(0, 2 * Z - 1)], send.at[7 + which])

    sweep_all(sall, got_one, one_recv, s_recv, send.at[9], True, False, lambda g: None)
    for t in range(STAGES):
        read_start(t)
    acc[...] = jnp.zeros_like(acc)
    low_acc[...] = jnp.zeros_like(low_acc)
    left(iall.at[pl.ds(0, 2 * (NO - 1))], send.at[4])
    grown = own_total(part, got_one, one_recv)
    degree[...] = own_total(line_part, line_got, line_recv)
    grown = grown / degree[...]
    gall[0] = grown
    gather_start(GROWN_AHEAD, gall.at[0], gall, g_recv, send.at[10], forward.at[3])
    gram_send(0, grown)
    left(part.at[pl.ds(0, Z - 1)], send.at[9])
    left(line_part.at[pl.ds(0, Z - 1)], send.at[3])

    def turn_first(g):
        @pl.when(g == NB // 8 - 1)
        def _():
            gram_turn(0)

    sweep_all(gall, got_two, two_recv, g_recv, send.at[11], False, True, turn_first)
    first = inverse_factor(gram_total(0))
    grown_two = own_total(part, got_two, two_recv) / degree[...]
    grown_two = jnp.dot(first, grown_two, precision=lax.Precision.HIGHEST, preferred_element_type=F32)
    gram_send(1, grown_two)
    gather_end(gall, send.at[10], forward.at[3])
    left(part.at[pl.ds(0, Z - 1)], send.at[11])
    gram_end(0)
    gram_turn(1)
    second = inverse_factor(gram_total(1))
    out[...] = jnp.dot(second, grown_two, precision=lax.Precision.HIGHEST, preferred_element_type=F32)
    gram_end(1)


def solution(mesh):
    X = math.isqrt(mesh.shape["row"] // 2)
    Z = mesh.shape["col"]
    NO, NB = X * X, 2 * X * X

    def step(frames, start):
        F, B = frames.shape
        V = start.shape[0]
        R = Z * B
        near, far = len(KEPT) * (NB // 8), len(SENT) * (NB // 8)
        vmem = pl.BlockSpec(memory_space=pltpu.VMEM)
        hbm = pl.BlockSpec(memory_space=pltpu.HBM)
        dma = pltpu.SemaphoreType.DMA
        basis, _, _ = pl.pallas_call(
            lambda *refs: kernel(X, Z, *refs),
            out_shape=(
                jax.ShapeDtypeStruct((V, B), F32),
                jax.ShapeDtypeStruct((Z * far, B, B), BF),
                jax.ShapeDtypeStruct((Z * far, B, B), F8),
            ),
            in_specs=[vmem, vmem],
            out_specs=(vmem, hbm, hbm),
            scratch_shapes=[
                pltpu.VMEM((Z, near, B, B), BF),
                pltpu.VMEM((Z, near, B, B), F8),
                pltpu.VMEM((BLOCKS * Z, B, B), BF),
                pltpu.VMEM((BLOCKS * Z, B, B), F8),
                pltpu.VMEM((Z, F, B), F32),
                pltpu.VMEM((NB, F, B), F32),
                pltpu.VMEM((NB, V, B), F32),
                pltpu.VMEM((NB, V, B), F32),
                pltpu.VMEM((NB, 1, B), F32),
                pltpu.VMEM((256, R), BF),
                pltpu.VMEM((B, 256), BF),
                pltpu.VMEM((2 * V + 16, R), F32),
                pltpu.VMEM((V, R), F32),
                pltpu.VMEM((8, R), F32),
                pltpu.VMEM((Z, V, B), F32),
                pltpu.VMEM((Z, 1, B), F32),
                pltpu.VMEM((2, Z, 1, B), F32),
                pltpu.VMEM((Z, 1, B), F32),
                pltpu.VMEM((Z, V, B), F32),
                pltpu.VMEM((Z, V, B), F32),
                pltpu.VMEM((1, B), F32),
                pltpu.VMEM((2, NO, 8, V * V // 8), F32),
                pltpu.VMEM((2, 2 * Z, 8, V * V // 8), F32),
                dma((NB,)), dma((NB,)), dma((NB,)),
                dma((Z,)), dma((2, Z)), dma((Z,)), dma((NO,)), dma((Z,)), dma((Z,)),
                dma((2, NO)), dma((2, 2 * Z)),
                dma((12,)), dma((4,)), dma((BLOCKS * Z, 2)), dma((BLOCKS * Z, 2)),
            ],
            compiler_params=pltpu.CompilerParams(
                collective_id=0, has_side_effects=True, vmem_limit_bytes=64 * 1024 * 1024 - 512 * 1024
            ),
            name="diffusion",
        )(frames, start)
        return basis

    return jax.shard_map(
        step,
        mesh=mesh,
        in_specs=(P(None, ("row", "col")), P(None, ("row", "col"))),
        out_specs=P(None, ("row", "col")),
        check_vma=False,
    )
```
